256 devices in a mesh: leaf: 64 (over z, y, core), panel: 4 (over x).
Axes of the slice: x: 4, y: 4, z: 8, core: 2. Of those that a mesh axis runs over, the one named last changes fastest.
Arguments:
- right_sides: float32 [7, 4096, 512], P(None, 'leaf', 'panel'), may hold values from -11 to 11
- inverse_diagonal: bfloat16 [7, 4096, 4096], P(None, 'leaf'), may hold values from -1 to 2, as said below
- off_diagonal: bfloat16 [6, 4096, 4096], P(None, 'leaf'), may hold values from -0.0625 to 0.0625
- structure: int32 [6, 32], replicated, may hold values from 0 to 95, as said below
- pivot_counts: int32 [7], replicated, may hold values from 2048 to 4096, as said below
Outputs:
- samples: float32 [7, 4096, 512], P(None, 'leaf', 'panel')
- sample_power: float32 [7, 4096], P(None, 'leaf')
The draws below stay inside these ranges and needn't reach their ends.
Inputs may be any that keep to these rules, and one draw needn't show every extreme that they name: `inverse_diagonal`: zero below the diagonal; diagonal entries positive. `structure`: a front of the middle level lists 4096 // 128 distinct blocks of the root (numbers below 32); a bottom front lists distinct blocks of the root and of its parent (parent p = 1 + (f - 3) // 2 holds block numbers p * 32 to (p + 1) * 32 - 1). `pivot_counts`: rows from the count on are padding; some front has exactly 4096 live rows and some exactly 2048.
All inputs are finite; a program needn't handle non-finite values.
Results may differ from the reference program's by a relative error of at most 0.0038.
Values may be sent and summed in bfloat16 or wider, within the bound.
No kernel may reach another device: no remote copies, remote signals or barrier semaphores. Data moves between devices by JAX's collectives and lax.ppermute only.
A program may use at most 64 MiB of HBM per device.

```python
import math
import jax
import jax.numpy as jnp
from jax import lax

S = 4096
K = 4096
BLK = 128
RHS = 512


def draw_right_sides(key, part):
    column_scale = 0.5 + jnp.arange(RHS, dtype=jnp.float32) / jnp.float32(max(RHS - 1, 1))
    values = jax.random.normal(jax.random.fold_in(key, 5), (7, S, RHS), jnp.float32)
    result = jnp.clip(values, -6.0, 6.0) * column_scale[None, None, :]
    return result


def draw_inverse_diagonal(key, part):
    row_ids = jnp.arange(S, dtype=jnp.int32)[:, None]
    col_ids = jnp.arange(S, dtype=jnp.int32)[None, :]
    upper = (col_ids > row_ids)[None, :, :]
    on_diag = (col_ids == row_ids)[None, :, :]
    spread = jnp.clip(jax.random.normal(jax.random.fold_in(key, 8), (7, S, S), jnp.float32), -6.0, 6.0) * (0.5 / math.sqrt(S))
    diag_part = jax.random.uniform(jax.random.fold_in(key, 9), (7, S, S), jnp.float32, 0.5, 1.5)
    return jnp.where(on_diag, diag_part, jnp.where(upper, spread, 0.0)).astype(jnp.bfloat16)


def draw_structure(key, part):
    root_blocks = S // BLK
    list_length = K // BLK
    lists = []
    for front_index in range(1, 7):
        front_key = jax.random.fold_in(key, 100 + front_index)
        if front_index <= 2:
            chosen = jax.random.permutation(front_key, root_blocks)[:list_length]
            if front_index == 1:
                present = jnp.any(chosen == 0)
                chosen = chosen.at[0].set(jnp.where(present, chosen[0], 0))
        else:
            parent = 1 + (front_index - 3) // 2
            picks = jax.random.permutation(front_key, 2 * root_blocks)[:list_length]
            if front_index == 6:
                top_pick = 2 * root_blocks - 1
                present = jnp.any(picks == top_pick)
                picks = picks.at[0].set(jnp.where(present, picks[0], top_pick))
            chosen = jnp.where(picks < root_blocks, picks, parent * root_blocks + picks - root_blocks)
        lists.append(chosen.astype(jnp.int32))
    return jnp.stack(lists, axis=0).astype(jnp.int32)


def draw_pivot_counts(key, part):
    order = jax.random.permutation(jax.random.fold_in(key, 11), 7)
    counts = jax.random.randint(jax.random.fold_in(key, 12), (7,), S // 2, S + 1, jnp.int32)
    front_ids = jnp.arange(7, dtype=jnp.int32)
    counts = jnp.where(front_ids == order[0], S, counts)
    counts = jnp.where(front_ids == order[1], S // 2, counts)
    return counts.astype(jnp.int32)


def block_levels(key, shape, shards, least, top_value):
    def one(dim, parts):
        steps = jax.random.uniform(jax.random.fold_in(jax.random.fold_in(key, 6), dim), (parts,), jnp.float32, least / len(shards), top_value / len(shards))
        return jnp.repeat(jnp.exp(steps), shape[dim] // parts).reshape((-1,) + (1,) * (len(shape) - dim - 1))

    gain = one(*shards[0])
    for cut in shards[1:]:
        gain = gain * one(*cut)
    return gain


def centred(own_key, dims, scale, reach, split=(), kind=jnp.bfloat16):
    level = block_levels(own_key, dims, split, -0.22, 0.18) if split else 1.0
    values = jax.random.normal(own_key, dims, jnp.float32) * scale * level
    return jnp.minimum(jnp.maximum(values, -reach), reach).astype(kind)


def setup_inputs(seed: int = 0) -> dict:
    arg_keys = jax.random.split(jax.random.key(seed), 6)
    right_sides = draw_right_sides(jax.random.fold_in(arg_keys[5], 71), 0)
    inverse_diagonal = draw_inverse_diagonal(jax.random.fold_in(arg_keys[5], 71), 0)
    off_diagonal = centred(arg_keys[2], (6, S, K), (2 * K) ** -0.5, 0.0625, ((1, 64),))
    structure = draw_structure(jax.random.fold_in(arg_keys[5], 71), 0)
    pivot_counts = draw_pivot_counts(jax.random.fold_in(arg_keys[5], 71), 0)
    return dict(right_sides=right_sides, inverse_diagonal=inverse_diagonal, off_diagonal=off_diagonal, structure=structure, pivot_counts=pivot_counts)


def product(left, right):
    return jnp.dot(left.astype(jnp.float32), right.astype(jnp.float32), precision=lax.Precision.HIGHEST, preferred_element_type=jnp.float32)


def reference(right_sides, inverse_diagonal, off_diagonal, structure, pivot_counts):
    row_index = (structure[:, :, None] * BLK + jnp.arange(BLK, dtype=jnp.int32)[None, None, :]).reshape(6, K).astype(jnp.int32)
    position = jnp.arange(S, dtype=jnp.int32)
    solved = []
    stored = []
    for front_index in range(7):
        live_mask = (position < pivot_counts[front_index]).astype(jnp.float32)[:, None]
        if front_index == 0:
            update = jnp.zeros((S, RHS), jnp.float32)
        else:
            ancestors = jnp.concatenate(stored, axis=0)
            picked = jnp.take(ancestors, row_index[front_index - 1], axis=0)
            update = product(off_diagonal[front_index - 1], picked)
        reduced = (live_mask * (right_sides[front_index] - update)).astype(jnp.bfloat16)
        solved_field = live_mask * product(inverse_diagonal[front_index], reduced)
        solved.append(solved_field)
        stored.append(solved_field.astype(jnp.bfloat16))
    samples = jnp.stack(solved, axis=0)
    sample_power = jnp.sum(samples * samples, axis=2) / jnp.float32(RHS)
    return samples, sample_power
```

```python
import jax
import jax.numpy as jnp
from jax import lax
from jax.experimental import pallas as pl
from jax.experimental.pallas import tpu as pltpu
from jax.sharding import PartitionSpec as P

NZ, NY, NC = 8, 4, 2
BF, F32 = jnp.bfloat16, jnp.float32
GRANT = 12 << 20


def place(z, y, c):
    return (z * NY + y) * NC + c


Z_GROUPS = [[place(z, y, c) for z in range(NZ)] for y in range(NY) for c in range(NC)]
Y_GROUPS = [[place(z, y, c) for y in range(NY)] for z in range(NZ) for c in range(NC)]
ZY_GROUPS = [[place(z, y, c) for z in range(NZ) for y in range(NY)] for c in range(NC)]
PARTNER = [(i, i ^ 1) for i in range(NZ * NY * NC)]


def spread(copies, groups):
    return lax.all_to_all(copies, "leaf", 0, 0, tiled=True, axis_index_groups=groups)


def with_partner(own):
    return own, lax.ppermute(own, "leaf", PARTNER)


def gather_once(copies):
    got = spread(copies, ZY_GROUPS)
    return with_partner(got.reshape(NZ * NY, 1, *got.shape[1:]))


def gather_twice(copies):
    line = spread(copies, Z_GROUPS)
    plane = spread(jnp.broadcast_to(line[None], (NY, *line.shape)), Y_GROUPS)
    return with_partner(plane)


def block_of(ref, j, row, rows):
    if ref.shape[1] == 1:
        return ref[j, 0, pl.ds(row, rows), :]
    return ref[lax.rem(j, NY), lax.div(j, NY), pl.ds(row, rows), :]


def live(scal, front, shape):
    position = lax.broadcasted_iota(jnp.int32, shape, 0) + scal[1]
    return position < scal[2 + front]


def put(picked, k, core, own, other):
    half = own.shape[0]
    base = k * (2 * half)
    picked[pl.ds(pl.multiple_of(base + core * half, half), half), :] = own
    picked[pl.ds(pl.multiple_of(base + (1 - core) * half, half), half), :] = other


def fetch(source, base, held, sem):
    copies = [
        pltpu.make_async_copy(source.at[base + f], held.at[f], sem.at[f]) for f in range(held.shape[0])
    ]
    for copy in copies:
        copy.start()
    return copies


def solve_kernel(fronts, first, copies, scal, own, other, inverse, out, *rest):
    sent, picked, held, sem = rest if copies else (None, *rest)
    rows = held.shape[1]
    core = scal[0]
    coming = fetch(inverse, first, held, sem)
    for f in range(fronts):
        @pl.loop(0, NZ * NY, unroll=4)
        def _(j):
            put(picked, j, core, block_of(own, j, f * rows, rows), block_of(other, j, f * rows, rows))

        coming[f].wait()
        running = jnp.dot(held[f], picked[...], preferred_element_type=F32)
        solved = jnp.where(live(scal, first + f, running.shape), running, 0.0)
        out[f] = solved
        if copies:
            small = solved.astype(BF)
            for n in range(copies):
                sent[n, f * rows : (f + 1) * rows, :] = small


def reduce_kernel(fronts, first, copies, scal, structure, root, root_other, *rest):
    if first >= 3:
        mid, mid_other, blocks, rhs, sent, picked, held, sem, sides, sides_sem = rest
    else:
        blocks, rhs, sent, picked, held, sem, sides, sides_sem = rest
    rows = held.shape[1]
    coming = fetch(blocks, first - 1, held, sem)
    sides_coming = fetch(rhs, first, sides, sides_sem)
    core = scal[0]
    n_root = NZ * NY
    for f in range(fronts):
        front = first + f

        @pl.loop(0, n_root, unroll=4)
        def _(k):
            b = structure[front - 1, k]
            j = jnp.clip(b, 0, n_root - 1)
            if first < 3:
                put(picked, k, core, block_of(root, j, 0, rows), block_of(root_other, j, 0, rows))
            else:
                parent = 1 + (front - 3) // 2
                at = (parent - 1) * rows
                i = jnp.clip(b - parent * n_root, 0, n_root - 1)

                @pl.when(b < n_root)
                def _():
                    put(picked, k, core, block_of(root, j, 0, rows), block_of(root_other, j, 0, rows))

                @pl.when(b >= n_root)
                def _():
                    put(picked, k, core, block_of(mid, i, at, rows), block_of(mid_other, i, at, rows))

        coming[f].wait()
        sides_coming[f].wait()
        update = jnp.dot(held[f], picked[...], preferred_element_type=F32)
        small = jnp.where(live(scal, front, update.shape), sides[f] - update, 0.0).astype(BF)
        for n in range(copies):
            sent[n, f * rows : (f + 1) * rows, :] = small


VMEM, SMEM = pl.BlockSpec(memory_space=pltpu.VMEM), pl.BlockSpec(memory_space=pltpu.SMEM)
ANY = pl.BlockSpec(memory_space=pl.ANY)


def on_chip(arrays):
    return [pltpu.with_memory_space_constraint(a, pltpu.VMEM) for a in arrays]


def solve(scal, gathered, inverse, first, fronts, copies):
    _, rows, width = inverse.shape
    columns = gathered[0].shape[-1]
    outs = [jax.ShapeDtypeStruct((fronts, rows, columns), F32)]
    if copies:
        outs.append(jax.ShapeDtypeStruct((copies, fronts * rows, columns), BF))

    def body(*refs):
        solve_kernel(fronts, first, copies, *refs)

    return pl.pallas_call(
        body,
        out_shape=outs,
        in_specs=[SMEM, VMEM, VMEM, ANY],
        out_specs=[VMEM] * len(outs),
        scratch_shapes=[
            pltpu.VMEM((width, columns), BF),
            pltpu.VMEM((fronts, rows, width), BF),
            pltpu.SemaphoreType.DMA((fronts,)),
        ],
        compiler_params=pltpu.CompilerParams(vmem_limit_bytes=GRANT),
        name=f"solve_{first}",
    )(scal, *on_chip(gathered), inverse)


def reduce(scal, structure, gathered, blocks, rhs, first, fronts, copies):
    _, rows, width = blocks.shape
    columns = rhs.shape[-1]

    def body(*refs):
        reduce_kernel(fronts, first, copies, *refs)

    return pl.pallas_call(
        body,
        out_shape=jax.ShapeDtypeStruct((copies, fronts * rows, columns), BF),
        in_specs=[SMEM, SMEM] + [VMEM] * len(gathered) + [ANY, ANY],
        out_specs=VMEM,
        scratch_shapes=[
            pltpu.VMEM((width, columns), BF),
            pltpu.VMEM((fronts, rows, width), BF),
            pltpu.SemaphoreType.DMA((fronts,)),
            pltpu.VMEM((fronts, rows, columns), F32),
            pltpu.SemaphoreType.DMA((fronts,)),
        ],
        compiler_params=pltpu.CompilerParams(vmem_limit_bytes=GRANT),
        name=f"reduce_{first}",
    )(scal, structure, *on_chip(gathered), blocks, rhs)


def local(right_sides, inverse_diagonal, off_diagonal, structure, pivot_counts):
    rows = right_sides.shape[1]
    columns = right_sides.shape[2]
    leaf = lax.axis_index("leaf")
    scal = jnp.concatenate([jnp.stack([leaf & 1, leaf * rows]).astype(jnp.int32), pivot_counts])
    live_root = (leaf * rows + jnp.arange(rows, dtype=jnp.int32) < pivot_counts[0]).astype(F32)[:, None]
    first = (live_root * right_sides[0]).astype(BF)
    n = NZ * NY
    root_sides = gather_once(jnp.broadcast_to(first[None], (n, rows, columns)))
    root, root_sent = solve(scal, root_sides, inverse_diagonal, 0, 1, n)
    root_all = gather_once(root_sent)
    sent = reduce(scal, structure, root_all, off_diagonal, right_sides, 1, 2, NZ)
    middle, middle_sent = solve(scal, gather_twice(sent), inverse_diagonal, 1, 2, NZ)
    middle_all = gather_twice(middle_sent)
    sent = reduce(scal, structure, root_all + middle_all, off_diagonal, right_sides, 3, 4, NZ)
    (bottom,) = solve(scal, gather_twice(sent), inverse_diagonal, 3, 4, 0)
    results = jnp.concatenate([root, middle, bottom], axis=0)
    mine = jnp.sum(results * results, axis=2)
    size = lax.axis_size("panel")
    a, b, c = (lax.ppermute(mine, "panel", [(i, i ^ d) for i in range(size)]) for d in (1, 2, 3))
    power = ((mine + a) + (b + c)) / F32(columns * size)
    return results, power


def solution(mesh):
    placed = (P(None, "leaf", "panel"), P(None, "leaf", None), P(None, "leaf", None), P(), P())
    return jax.shard_map(
        local,
        mesh=mesh,
        in_specs=placed,
        out_specs=(P(None, "leaf", "panel"), P(None, "leaf")),
        check_vma=False,
    )
```

```python
import jax
import jax.numpy as jnp
from jax import lax
from jax.experimental import pallas as pl
from jax.experimental.pallas import tpu as pltpu
from jax.sharding import PartitionSpec as P

NZ, NY, NC = 8, 4, 2
N = NZ * NY
BF, F32 = jnp.bfloat16, jnp.float32
GRANT = 16 << 20


def place(z, y, c):
    return (z % NZ * NY + y % NY) * NC + c


def pairs(move):
    return [
        (place(z, y, c), place(*move(z, y, c))) for z in range(NZ) for y in range(NY) for c in range(NC)
    ]


Z_GROUPS = [[place(z, y, c) for z in range(NZ)] for y in range(NY) for c in range(NC)]
ZY_GROUPS = [[place(z, y, c) for z in range(NZ) for y in range(NY)] for c in range(NC)]
PARTNER = pairs(lambda z, y, c: (z, y, 1 - c))
UP = pairs(lambda z, y, c: (z, y + 1, c))
DOWN = pairs(lambda z, y, c: (z, y - 1, c))


def spread(copies, groups):
    return lax.all_to_all(copies, "leaf", 0, 0, tiled=True, axis_index_groups=groups)


def send(x, to):
    return lax.ppermute(x, "leaf", to)


def gather_once(copies):
    own = spread(copies, ZY_GROUPS)
    return [(own, send(own, PARTNER), lambda y: list(range(N)))]


def line_at(shift, start, stop):
    return lambda y: [z * NY + lax.rem(y + shift, NY) for z in range(start, stop)]


def gather_twice(copies):
    line = spread(copies, Z_GROUPS)
    below, above = send(line, UP), send(line, DOWN)
    half = NZ // 2
    far_a, far_b = send(below[:half], UP), send(above[half:], DOWN)
    return [
        (line, send(line, PARTNER), line_at(0, 0, NZ)),
        (below, send(below, PARTNER), line_at(NY - 1, 0, NZ)),
        (above, send(above, PARTNER), line_at(1, 0, NZ)),
        (far_a, send(far_a, PARTNER), line_at(2, 0, half)),
        (far_b, send(far_b, PARTNER), line_at(2, half, NZ)),
    ]


def assemble(dest, base, core, y, parts, row, rows):
    for own, other, blocks in parts:
        for i, j in enumerate(blocks(y)):
            at = base + j * (2 * rows)
            dest[pl.ds(pl.multiple_of(at + core * rows, rows), rows), :] = own[i, row : row + rows, :]
            dest[pl.ds(pl.multiple_of(at + (1 - core) * rows, rows), rows), :] = other[i, row : row + rows, :]


def live(scal, front, shape):
    position = lax.broadcasted_iota(jnp.int32, shape, 0) + scal[1]
    return position < scal[3 + front]


def share(sent, f, value):
    rows = value.shape[0]
    small = value.astype(BF)
    for n in range(sent.shape[0]):
        sent[n, f * rows : (f + 1) * rows, :] = small


def root_kernel(blocks, scal, own, other, inverse, out, sent, held, picked, sem):
    rows = held.shape[0]
    copy = pltpu.make_async_copy(inverse.at[0], held, sem)
    copy.start()
    assemble(picked, 0, scal[0], scal[2], [(own, other, blocks)], 0, rows)
    copy.wait()
    running = jnp.dot(held[...], picked[...], preferred_element_type=F32)
    solved = jnp.where(live(scal, 0, running.shape), running, 0.0)
    out[0] = solved
    share(sent, 0, solved)


def solve_kernel(fronts, first, blocks, scal, *refs):
    n = 2 * len(blocks)
    parts = [(refs[2 * i], refs[2 * i + 1], b) for i, b in enumerate(blocks)]
    inverse, out, *sent, picked = refs[n:]
    rows, width = inverse.shape[1], inverse.shape[2]
    for f in range(fronts):
        assemble(picked, f * width, scal[0], scal[2], parts, f * rows, rows)
        running = jnp.dot(inverse[first + f], picked[f * width : (f + 1) * width, :], preferred_element_type=F32)
        solved = jnp.where(live(scal, first + f, running.shape), running, 0.0)
        out[f] = solved
        if sent:
            share(sent[0], f, solved)


def reduced(scal, structure, front, stack, picked, matrix, rhs):
    count = structure.shape[1]
    size = picked.shape[0] // count
    for k in range(count):
        at = pl.multiple_of(structure[front - 1, k] * size, size)
        picked[k * size : (k + 1) * size, :] = stack[pl.ds(at, size), :]
    update = jnp.dot(matrix[front - 1], picked[...], preferred_element_type=F32)
    return jnp.where(live(scal, front, update.shape), rhs[front] - update, 0.0)


def middle_kernel(blocks, scal, structure, own, other, matrix, rhs, sent, root, picked):
    rows = matrix.shape[1]
    assemble(root, 0, scal[0], scal[2], [(own, other, blocks)], 0, rows)
    for f in range(2):
        share(sent, f, reduced(scal, structure, 1 + f, root, picked.at[f], matrix, rhs))


def bottom_kernel(blocks, scal, structure, root, *refs):
    n = 2 * len(blocks)
    parts = [(refs[2 * i], refs[2 * i + 1], b) for i, b in enumerate(blocks)]
    matrix, rhs, sent, stack, picked = refs[n:]
    rows, width = matrix.shape[1], matrix.shape[2]
    stack[0:width, :] = root[...]
    for m in range(2):
        assemble(stack, (1 + m) * width, scal[0], scal[2], parts, m * rows, rows)
        for f in (2 * m, 2 * m + 1):
            share(sent, f, reduced(scal, structure, 3 + f, stack, picked.at[f], matrix, rhs))


VMEM, SMEM = pl.BlockSpec(memory_space=pltpu.VMEM), pl.BlockSpec(memory_space=pltpu.SMEM)
ANY = pl.BlockSpec(memory_space=pl.ANY)


def on_chip(*arrays):
    return [pltpu.with_memory_space_constraint(a, pltpu.VMEM) for a in arrays]


def call(name, body, specs, args, shapes, scratch):
    return pl.pallas_call(
        body,
        out_shape=[jax.ShapeDtypeStruct(s, d) for s, d in shapes],
        in_specs=specs,
        out_specs=[VMEM] * len(shapes),
        scratch_shapes=scratch,
        compiler_params=pltpu.CompilerParams(vmem_limit_bytes=GRANT),
        name=name,
    )(*args)


def flat(gathered):
    return on_chip(*(a for own, other, _ in gathered for a in (own, other)))


def local(right_sides, inverse_diagonal, off_diagonal, structure, pivot_counts):
    rows, columns = right_sides.shape[1:]
    width = inverse_diagonal.shape[2]
    leaf = lax.axis_index("leaf").astype(jnp.int32)
    place_here = jnp.stack([leaf % NC, leaf * rows, leaf // NC % NY])
    scal = jnp.concatenate([place_here, pivot_counts])
    live_root = (leaf * rows + jnp.arange(rows, dtype=jnp.int32) < pivot_counts[0]).astype(F32)[:, None]
    first = (live_root * right_sides[0]).astype(BF)

    got = gather_once(jnp.broadcast_to(first[None], (N, rows, columns)))
    blocks = got[0][2]
    root, sent = call(
        "root",
        lambda *refs: root_kernel(blocks, *refs),
        [SMEM, VMEM, VMEM, ANY],
        (scal, *flat(got), pltpu.with_memory_space_constraint(inverse_diagonal, pltpu.HBM)),
        [((1, rows, columns), F32), ((N, rows, columns), BF)],
        [pltpu.VMEM((rows, width), BF), pltpu.VMEM((width, columns), BF), pltpu.SemaphoreType.DMA(())],
    )
    got = gather_once(sent)
    inverse, matrix, sides = on_chip(inverse_diagonal, off_diagonal, right_sides)
    sent, root_all = call(
        "middle_sides",
        lambda *refs: middle_kernel(blocks, *refs),
        [SMEM, SMEM] + [VMEM] * 4,
        (scal, structure, *flat(got), matrix, sides),
        [((NZ, 2 * rows, columns), BF), ((width, columns), BF)],
        [pltpu.VMEM((2, width, columns), BF)],
    )
    got = gather_twice(sent)
    blocks = [b for _, _, b in got]
    middle, sent = call(
        "middle",
        lambda *refs: solve_kernel(2, 1, blocks, *refs),
        [SMEM] + [VMEM] * (2 * len(got) + 1),
        (scal, *flat(got), inverse),
        [((2, rows, columns), F32), ((NZ, 2 * rows, columns), BF)],
        [pltpu.VMEM((2 * width, columns), BF)],
    )
    got = gather_twice(sent)
    (sent,) = call(
        "bottom_sides",
        lambda *refs: bottom_kernel(blocks, *refs),
        [SMEM, SMEM] + [VMEM] * (2 * len(got) + 3),
        (scal, structure, *on_chip(root_all), *flat(got), matrix, sides),
        [((NZ, 4 * rows, columns), BF)],
        [pltpu.VMEM((3 * width, columns), BF), pltpu.VMEM((4, width, columns), BF)],
    )
    got = gather_twice(sent)
    (bottom,) = call(
        "bottom",
        lambda *refs: solve_kernel(4, 3, blocks, *refs),
        [SMEM] + [VMEM] * (2 * len(got) + 1),
        (scal, *flat(got), inverse),
        [((4, rows, columns), F32)],
        [pltpu.VMEM((4 * width, columns), BF)],
    )
    results = jnp.concatenate([root, middle, bottom], axis=0)
    mine = jnp.sum(results * results, axis=2)
    size = lax.axis_size("panel")
    a, b, c = (lax.ppermute(mine, "panel", [(i, i ^ d) for i in range(size)]) for d in (1, 2, 3))
    power = ((mine + a) + (b + c)) / F32(columns * size)
    return results, power


def solution(mesh):
    placed = (P(None, "leaf", "panel"), P(None, "leaf", None), P(None, "leaf", None), P(), P())
    return jax.shard_map(
        local,
        mesh=mesh,
        in_specs=placed,
        out_specs=(P(None, "leaf", "panel"), P(None, "leaf")),
        check_vma=False,
    )
```

```python
import jax
import jax.numpy as jnp
from jax import lax
from jax.experimental import pallas as pl
from jax.experimental.pallas import tpu as pltpu
from jax.sharding import PartitionSpec as P

NZ, NY, NC = 8, 4, 2
N = NZ * NY
BF, F32 = jnp.bfloat16, jnp.float32
GRANT = 16 << 20


def place(z, y, c):
    return (z % NZ * NY + y % NY) * NC + c


def pairs(move):
    return [
        (place(z, y, c), place(*move(z, y, c))) for z in range(NZ) for y in range(NY) for c in range(NC)
    ]


Z_GROUPS = [[place(z, y, c) for z in range(NZ)] for y in range(NY) for c in range(NC)]
PARTNER = pairs(lambda z, y, c: (z, y, 1 - c))
NEAR = pairs(lambda z, y, c: (z, y ^ 1, c))
NEXT = pairs(lambda z, y, c: (z, y ^ 3, c))
FAR = pairs(lambda z, y, c: (z, y ^ 2, c))


def send(x, to):
    return lax.ppermute(x, "leaf", to)


def chips(flip, start=0, stop=NZ):
    return lambda y: [z * NY + jnp.bitwise_xor(y, flip) for z in range(start, stop)]


def gather(copies, relay):
    line = lax.all_to_all(copies, "leaf", 0, 0, tiled=True, axis_index_groups=Z_GROUPS)
    half = NZ // 2
    if relay:
        near, side = send(line, NEAR), send(line, NEXT)
        far = [(send(near[:half], NEXT), chips(2, 0, half)), (send(side[half:], NEAR), chips(2, half, NZ))]
        got = [(line, chips(0)), (near, chips(1)), (side, chips(3))] + far
        return [(own, send(own, PARTNER), at) for own, at in got]
    far = send(line, FAR)
    swapped = send(line, PARTNER)
    near, side = send(line, NEAR), send(line, NEXT)
    return [
        (line, swapped, chips(0)),
        (near, send(near, PARTNER), chips(1)),
        (side, send(side, PARTNER), chips(3)),
        (far, send(far, PARTNER), chips(2)),
    ]


def assemble(dest, base, leaf, parts, row, rows):
    core, y = leaf[0] & (NC - 1), (leaf[0] >> 1) & (NY - 1)
    for own, other, blocks in parts:
        for i, j in enumerate(blocks(y)):
            at = base + j * (2 * rows)
            dest[pl.ds(pl.multiple_of(at + core * rows, rows), rows), :] = own[i, row : row + rows, :]
            dest[pl.ds(pl.multiple_of(at + (1 - core) * rows, rows), rows), :] = other[i, row : row + rows, :]


def live(leaf, counts, front, shape):
    position = lax.broadcasted_iota(jnp.int32, shape, 0) + leaf[0] * shape[0]
    return position < counts[front]


def share(sent, f, value):
    rows = value.shape[0]
    small = value.astype(BF)
    for n in range(sent.shape[0]):
        sent[n, f * rows : (f + 1) * rows, :] = small


def row_power(x):
    return jnp.sum((x * x).T, axis=0, keepdims=True)


def solve(f, front, leaf, counts, parts, matrix, picked):
    rows, width = matrix.shape
    assemble(picked, f * width, leaf, parts, f * rows, rows)
    running = jnp.dot(matrix[...], picked[f * width : (f + 1) * width, :], preferred_element_type=F32)
    return jnp.where(live(leaf, counts, front, running.shape), running, 0.0)


def split(refs, blocks):
    n = 2 * len(blocks)
    return [(refs[2 * i], refs[2 * i + 1], b) for i, b in enumerate(blocks)], refs[n:]


def first_kernel(leaf, counts, sides, inverse, sent, held, mine, sems):
    copies = [
        pltpu.make_async_copy(sides.at[0], mine, sems.at[0]),
        pltpu.make_async_copy(inverse.at[0:1], held, sems.at[1]),
    ]
    for copy in copies:
        copy.start()
    copies[0].wait()
    share(sent, 0, jnp.where(live(leaf, counts, 0, mine.shape), mine[...], 0.0))
    copies[1].wait()


def upper_kernel(fronts, first, at, blocks, leaf, counts, *refs):
    parts, (inverse, out, sent, picked) = split(refs, blocks)
    for f in range(fronts):
        solved = solve(f, first + f, leaf, counts, parts, inverse.at[at + f], picked)
        out[f] = solved
        share(sent, f, solved)


def last_kernel(blocks, leaf, counts, root, middle, *refs):
    parts, (inverse, out, power, picked) = split(refs, blocks)
    n = root.shape[0] + middle.shape[0]
    for f in range(n):
        done = root[0] if f == 0 else middle[f - 1]
        out[f] = done
        power[f : f + 1, :] = row_power(done)
    for f in range(out.shape[0] - n):
        solved = solve(f, n + f, leaf, counts, parts, inverse.at[n + f], picked)
        out[n + f] = solved
        power[n + f : n + f + 1, :] = row_power(solved)


def reduced(leaf, counts, structure, front, stack, picked, matrix, rhs):
    count = structure.shape[1]
    size = picked.shape[0] // count
    for k in range(count):
        at = pl.multiple_of(structure[front - 1, k] * size, size)
        picked[k * size : (k + 1) * size, :] = stack[pl.ds(at, size), :]
    update = jnp.dot(matrix[front - 1], picked[...], preferred_element_type=F32)
    return jnp.where(live(leaf, counts, front, update.shape), rhs[front] - update, 0.0)


def middle_kernel(blocks, leaf, counts, structure, *refs):
    parts, (matrix, rhs, sent, root, picked) = split(refs, blocks)
    rows = matrix.shape[1]
    assemble(root, 0, leaf, parts, 0, rows)
    for f in range(2):
        share(sent, f, reduced(leaf, counts, structure, 1 + f, root, picked.at[f], matrix, rhs))


def bottom_kernel(blocks, leaf, counts, structure, root, *refs):
    parts, (matrix, rhs, sent, stack, picked) = split(refs, blocks)
    rows, width = matrix.shape[1], matrix.shape[2]
    stack[0:width, :] = root[...]
    for m in range(2):
        assemble(stack, (1 + m) * width, leaf, parts, m * rows, rows)
        for f in (2 * m, 2 * m + 1):
            share(sent, f, reduced(leaf, counts, structure, 3 + f, stack, picked.at[f], matrix, rhs))


VMEM, SMEM = pl.BlockSpec(memory_space=pltpu.VMEM), pl.BlockSpec(memory_space=pltpu.SMEM)
ANY = pl.BlockSpec(memory_space=pl.ANY)


def on_chip(*arrays):
    return [pltpu.with_memory_space_constraint(a, pltpu.VMEM) for a in arrays]


def call(name, body, specs, args, shapes, scratch):
    return pl.pallas_call(
        body,
        out_shape=[jax.ShapeDtypeStruct(s, d) for s, d in shapes],
        in_specs=specs,
        out_specs=[VMEM] * len(shapes),
        scratch_shapes=scratch,
        compiler_params=pltpu.CompilerParams(vmem_limit_bytes=GRANT),
        name=name,
    )(*args)


def flat(gathered):
    return on_chip(*(a for own, other, _ in gathered for a in (own, other)))


def local(right_sides, inverse_diagonal, off_diagonal, structure, pivot_counts):
    rows, columns = right_sides.shape[1:]
    width = inverse_diagonal.shape[2]
    leaf = lax.axis_index("leaf").astype(jnp.int32)[None]
    inverse, matrix, sides = on_chip(inverse_diagonal, off_diagonal, right_sides)
    far = [pltpu.with_memory_space_constraint(a, pltpu.HBM) for a in (right_sides, inverse_diagonal)]

    def upper(name, got, fronts, first, source, at):
        return call(
            name,
            lambda *refs: upper_kernel(fronts, first, at, [b for _, _, b in got], *refs),
            [SMEM, SMEM] + [VMEM] * (2 * len(got) + 1),
            (leaf, pivot_counts, *flat(got), source),
            [((fronts, rows, columns), F32), ((NZ, fronts * rows, columns), BF)],
            [pltpu.VMEM((fronts * width, columns), BF)],
        )

    sent, held = call(
        "first",
        first_kernel,
        [SMEM, SMEM, ANY, ANY],
        (leaf, pivot_counts, *far),
        [((NZ, rows, columns), BF), ((1, rows, width), BF)],
        [pltpu.VMEM((rows, columns), F32), pltpu.SemaphoreType.DMA((2,))],
    )
    root, sent = upper("root", gather(sent, False), 1, 0, *on_chip(held), 0)
    got = gather(sent, False)
    sent, root_all = call(
        "middle_sides",
        lambda *refs: middle_kernel([b for _, _, b in got], *refs),
        [SMEM, SMEM, SMEM] + [VMEM] * (2 * len(got) + 2),
        (leaf, pivot_counts, structure, *flat(got), matrix, sides),
        [((NZ, 2 * rows, columns), BF), ((width, columns), BF)],
        [pltpu.VMEM((2, width, columns), BF)],
    )
    middle, sent = upper("middle", gather(sent, False), 2, 1, inverse, 1)
    got = gather(sent, False)
    (sent,) = call(
        "bottom_sides",
        lambda *refs: bottom_kernel([b for _, _, b in got], *refs),
        [SMEM, SMEM, SMEM] + [VMEM] * (2 * len(got) + 3),
        (leaf, pivot_counts, structure, *on_chip(root_all), *flat(got), matrix, sides),
        [((NZ, 4 * rows, columns), BF)],
        [pltpu.VMEM((3 * width, columns), BF), pltpu.VMEM((4, width, columns), BF)],
    )
    got = gather(sent, True)
    results, mine = call(
        "bottom",
        lambda *refs: last_kernel([b for _, _, b in got], *refs),
        [SMEM, SMEM] + [VMEM] * (2 * len(got) + 3),
        (leaf, pivot_counts, *on_chip(root, middle), *flat(got), inverse),
        [((7, rows, columns), F32), ((7, rows), F32)],
        [pltpu.VMEM((4 * width, columns), BF)],
    )
    size = lax.axis_size("panel")
    a, b, c = (lax.ppermute(mine, "panel", [(i, i ^ d) for i in range(size)]) for d in (1, 2, 3))
    power = ((mine + a) + (b + c)) / F32(columns * size)
    return results, power


def solution(mesh):
    placed = (P(None, "leaf", "panel"), P(None, "leaf", None), P(None, "leaf", None), P(), P())
    return jax.shard_map(
        local,
        mesh=mesh,
        in_specs=placed,
        out_specs=(P(None, "leaf", "panel"), P(None, "leaf")),
        check_vma=False,
    )
```

```python
import jax
import jax.numpy as jnp
from jax import lax
from jax.experimental import pallas as pl
from jax.experimental.pallas import tpu as pltpu
from jax.sharding import PartitionSpec as P

NZ, NY, NC = 8, 4, 2
N = NZ * NY
BF, F32 = jnp.bfloat16, jnp.float32
GRANT = 16 << 20


def place(z, y, c):
    return (z % NZ * NY + y % NY) * NC + c


def pairs(move):
    return [
        (place(z, y, c), place(*move(z, y, c))) for z in range(NZ) for y in range(NY) for c in range(NC)
    ]


Z_GROUPS = [[place(z, y, c) for z in range(NZ)] for y in range(NY) for c in range(NC)]
PARTNER = pairs(lambda z, y, c: (z, y, 1 - c))
UP = pairs(lambda z, y, c: (z, y + 1, c))
DOWN = pairs(lambda z, y, c: (z, y - 1, c))
NEAR = pairs(lambda z, y, c: (z, y ^ 1, c))
NEXT = pairs(lambda z, y, c: (z, y ^ 3, c))
FAR = pairs(lambda z, y, c: (z, y ^ 2, c))


def send(x, to):
    return lax.ppermute(x, "leaf", to)


def chips(away, start=0, stop=NZ):
    return lambda y: [z * NY + away(y) for z in range(start, stop)]


def flip(n):
    return lambda y: jnp.bitwise_xor(y, n)


def shift(n):
    return lambda y: (y + n) & (NY - 1)


def gather(copies, relay):
    line = lax.all_to_all(copies, "leaf", 0, 0, tiled=True, axis_index_groups=Z_GROUPS)
    half = NZ // 2
    if relay:
        below, above = send(line, UP), send(line, DOWN)
        got = [
            (line, chips(shift(0))),
            (below, chips(shift(-1))),
            (above, chips(shift(1))),
            (send(below[:half], UP), chips(shift(2), 0, half)),
            (send(above[half:], DOWN), chips(shift(2), half, NZ)),
        ]
    else:
        far = send(line, FAR)
        got = [
            (line, chips(flip(0))),
            (far, chips(flip(2))),
            (send(line, NEXT), chips(flip(3))),
            (send(line, NEAR), chips(flip(1))),
        ]
    return [(own, send(own, PARTNER), at) for own, at in got]


def assemble(dest, base, leaf, parts, row, rows):
    core, y = leaf[0] & (NC - 1), (leaf[0] >> 1) & (NY - 1)
    for own, other, blocks in parts:
        for i, j in enumerate(blocks(y)):
            at = base + j * (2 * rows)
            dest[pl.ds(pl.multiple_of(at + core * rows, rows), rows), :] = own[i, row : row + rows, :]
            dest[pl.ds(pl.multiple_of(at + (1 - core) * rows, rows), rows), :] = other[i, row : row + rows, :]


def live(leaf, counts, front, shape):
    position = lax.broadcasted_iota(jnp.int32, shape, 0) + leaf[0] * shape[0]
    return position < counts[front]


def share(sent, f, value):
    rows = value.shape[0]
    small = value.astype(BF)
    for n in range(sent.shape[0]):
        sent[n, f * rows : (f + 1) * rows, :] = small


def row_power(x):
    return jnp.sum((x * x).T, axis=0, keepdims=True)


def solve(f, front, leaf, counts, parts, matrix, picked):
    rows, width = matrix.shape
    assemble(picked, f * width, leaf, parts, f * rows, rows)
    running = jnp.dot(matrix[...], picked[f * width : (f + 1) * width, :], preferred_element_type=F32)
    return jnp.where(live(leaf, counts, front, running.shape), running, 0.0)


def split(refs, blocks):
    n = 2 * len(blocks)
    return [(refs[2 * i], refs[2 * i + 1], b) for i, b in enumerate(blocks)], refs[n:]


def first_kernel(leaf, far_counts, sides, inverse, sent, held, mine, counts, sems):
    copies = [
        pltpu.make_async_copy(far_counts, counts, sems.at[0]),
        pltpu.make_async_copy(sides.at[0], mine, sems.at[1]),
        pltpu.make_async_copy(inverse.at[0:1], held, sems.at[2]),
    ]
    for copy in copies:
        copy.start()
    copies[0].wait()
    copies[1].wait()
    share(sent, 0, jnp.where(live(leaf, counts, 0, mine.shape), mine[...], 0.0))
    copies[2].wait()


def upper_kernel(fronts, first, at, blocks, leaf, counts, *refs):
    parts, (inverse, out, sent, picked) = split(refs, blocks)
    for f in range(fronts):
        solved = solve(f, first + f, leaf, counts, parts, inverse.at[at + f], picked)
        out[f] = solved
        share(sent, f, solved)


def last_kernel(blocks, leaf, counts, root, middle, *refs):
    parts, (inverse, out, power, picked) = split(refs, blocks)
    n = root.shape[0] + middle.shape[0]
    for f in range(n):
        done = root[0] if f == 0 else middle[f - 1]
        out[f] = done
        power[f : f + 1, :] = row_power(done)
    for f in range(out.shape[0] - n):
        solved = solve(f, n + f, leaf, counts, parts, inverse.at[n + f], picked)
        out[n + f] = solved
        power[n + f : n + f + 1, :] = row_power(solved)


def reduced(leaf, counts, structure, front, stack, picked, matrix, rhs):
    count = structure.shape[1]
    size = picked.shape[0] // count
    for k in range(count):
        at = pl.multiple_of(structure[front - 1, k] * size, size)
        picked[k * size : (k + 1) * size, :] = stack[pl.ds(at, size), :]
    update = jnp.dot(matrix[front - 1], picked[...], preferred_element_type=F32)
    return jnp.where(live(leaf, counts, front, update.shape), rhs[front] - update, 0.0)


def middle_kernel(blocks, leaf, counts, structure, *refs):
    parts, (matrix, rhs, sent, root, picked) = split(refs, blocks)
    rows = matrix.shape[1]
    assemble(root, 0, leaf, parts, 0, rows)
    for f in range(2):
        share(sent, f, reduced(leaf, counts, structure, 1 + f, root, picked.at[f], matrix, rhs))


def bottom_kernel(blocks, leaf, counts, structure, root, *refs):
    parts, (matrix, rhs, sent, stack, picked) = split(refs, blocks)
    rows, width = matrix.shape[1], matrix.shape[2]
    stack[0:width, :] = root[...]
    for m in range(2):
        assemble(stack, (1 + m) * width, leaf, parts, m * rows, rows)
        for f in (2 * m, 2 * m + 1):
            share(sent, f, reduced(leaf, counts, structure, 3 + f, stack, picked.at[f], matrix, rhs))


VMEM, SMEM = pl.BlockSpec(memory_space=pltpu.VMEM), pl.BlockSpec(memory_space=pltpu.SMEM)
ANY = pl.BlockSpec(memory_space=pl.ANY)


def on_chip(*arrays):
    return [pltpu.with_memory_space_constraint(a, pltpu.VMEM) for a in arrays]


def call(name, body, specs, args, shapes, scratch):
    return pl.pallas_call(
        body,
        out_shape=[jax.ShapeDtypeStruct(s, d) for s, d in shapes],
        in_specs=specs,
        out_specs=[VMEM] * len(shapes),
        scratch_shapes=scratch,
        compiler_params=pltpu.CompilerParams(vmem_limit_bytes=GRANT),
        name=name,
    )(*args)


def flat(gathered):
    return on_chip(*(a for own, other, _ in gathered for a in (own, other)))


def local(right_sides, inverse_diagonal, off_diagonal, structure, pivot_counts):
    rows, columns = right_sides.shape[1:]
    width = inverse_diagonal.shape[2]
    leaf = lax.axis_index("leaf").astype(jnp.int32)[None]
    inverse, matrix, sides = on_chip(inverse_diagonal, off_diagonal, right_sides)
    far = [pltpu.with_memory_space_constraint(a, pltpu.HBM) for a in (pivot_counts, right_sides, inverse_diagonal)]

    def upper(name, got, fronts, first, source, at):
        return call(
            name,
            lambda *refs: upper_kernel(fronts, first, at, [b for _, _, b in got], *refs),
            [SMEM, SMEM] + [VMEM] * (2 * len(got) + 1),
            (leaf, pivot_counts, *flat(got), source),
            [((fronts, rows, columns), F32), ((NZ, fronts * rows, columns), BF)],
            [pltpu.VMEM((fronts * width, columns), BF)],
        )

    sent, held = call(
        "first",
        first_kernel,
        [SMEM, ANY, ANY, ANY],
        (leaf, *far),
        [((NZ, rows, columns), BF), ((1, rows, width), BF)],
        [pltpu.VMEM((rows, columns), F32), pltpu.SMEM((7,), jnp.int32), pltpu.SemaphoreType.DMA((3,))],
    )
    root, sent = upper("root", gather(sent, False), 1, 0, *on_chip(held), 0)
    got = gather(sent, False)
    sent, root_all = call(
        "middle_sides",
        lambda *refs: middle_kernel([b for _, _, b in got], *refs),
        [SMEM, SMEM, SMEM] + [VMEM] * (2 * len(got) + 2),
        (leaf, pivot_counts, structure, *flat(got), matrix, sides),
        [((NZ, 2 * rows, columns), BF), ((width, columns), BF)],
        [pltpu.VMEM((2, width, columns), BF)],
    )
    middle, sent = upper("middle", gather(sent, False), 2, 1, inverse, 1)
    got = gather(sent, False)
    (sent,) = call(
        "bottom_sides",
        lambda *refs: bottom_kernel([b for _, _, b in got], *refs),
        [SMEM, SMEM, SMEM] + [VMEM] * (2 * len(got) + 3),
        (leaf, pivot_counts, structure, *on_chip(root_all), *flat(got), matrix, sides),
        [((NZ, 4 * rows, columns), BF)],
        [pltpu.VMEM((3 * width, columns), BF), pltpu.VMEM((4, width, columns), BF)],
    )
    got = gather(sent, True)
    results, mine = call(
        "bottom",
        lambda *refs: last_kernel([b for _, _, b in got], *refs),
        [SMEM, SMEM] + [VMEM] * (2 * len(got) + 3),
        (leaf, pivot_counts, *on_chip(root, middle), *flat(got), inverse),
        [((7, rows, columns), F32), ((7, rows), F32)],
        [pltpu.VMEM((4 * width, columns), BF)],
    )
    size = lax.axis_size("panel")
    a, b, c = (lax.ppermute(mine, "panel", [(i, i ^ d) for i in range(size)]) for d in (1, 3, 2))
    power = ((mine + a) + (b + c)) / F32(columns * size)
    return results, power


def solution(mesh):
    placed = (P(None, "leaf", "panel"), P(None, "leaf", None), P(None, "leaf", None), P(), P())
    return jax.shard_map(
        local,
        mesh=mesh,
        in_specs=placed,
        out_specs=(P(None, "leaf", "panel"), P(None, "leaf")),
        check_vma=False,
    )
```
